32 devices in a mesh: shard: 8 (over z, y), tensor: 4 (over x, core).
Axes of the slice: x: 2, y: 2, z: 4, core: 2. Of those that a mesh axis runs over, the one named last changes fastest.
Arguments:
- attention_grad: bfloat16 [4, 768, 768], P(None, 'shard', 'tensor'), may hold values from -500 to 500
- up_grad: bfloat16 [768, 3072], P('shard', 'tensor'), may hold values from -500 to 500
- down_grad: bfloat16 [3072, 768], P('shard', 'tensor'), may hold values from -500 to 500
- attention_basis: float32 [4, 768, 256], P(None, 'shard'), may hold values from -0.21875 to 0.21875
- up_basis: float32 [768, 256], P('shard'), may hold values from -0.21875 to 0.21875
- down_basis: float32 [3072, 256], P('shard'), may hold values from -0.109375 to 0.109375
- attention_mean: float32 [4, 256, 768], P(None, 'shard', 'tensor'), may hold values from -1.8 to 1.8
- attention_power: float32 [4, 256, 768], P(None, 'shard', 'tensor'), may hold values from 0.05 to 1
- up_mean: float32 [256, 3072], P('shard', 'tensor'), may hold values from -1.8 to 1.8
- up_power: float32 [256, 3072], P('shard', 'tensor'), may hold values from 0.05 to 1
- down_mean: float32 [256, 768], P('shard', 'tensor'), may hold values from -1.8 to 1.8
- down_power: float32 [256, 768], P('shard', 'tensor'), may hold values from 0.05 to 1
- vector_grad: float32 [13, 768], P(None, ('shard', 'tensor')), may hold values from -6 to 6
- vector_mean: float32 [13, 768], P(None, ('shard', 'tensor')), may hold values from -1.8 to 1.8
- vector_power: float32 [13, 768], P(None, ('shard', 'tensor')), may hold values from 0.05 to 1
Outputs:
- step_attention: float32 [4, 768, 768], P(None, 'shard', 'tensor')
- step_up: float32 [768, 3072], P('shard', 'tensor')
- step_down: float32 [3072, 768], P('shard', 'tensor')
- mean_attention: float32 [4, 256, 768], P(None, 'shard', 'tensor')
- power_attention: float32 [4, 256, 768], P(None, 'shard', 'tensor')
- mean_up: float32 [256, 3072], P('shard', 'tensor')
- power_up: float32 [256, 3072], P('shard', 'tensor')
- mean_down: float32 [256, 768], P('shard', 'tensor')
- power_down: float32 [256, 768], P('shard', 'tensor')
- basis_attention: float32 [4, 768, 256], P(None, 'shard')
- basis_up: float32 [768, 256], P('shard')
- basis_down: float32 [3072, 256], P('shard')
- step_vector: float32 [13, 768], P(None, ('shard', 'tensor'))
- mean_vector: float32 [13, 768], P(None, ('shard', 'tensor'))
- power_vector: float32 [13, 768], P(None, ('shard', 'tensor'))
The draws below stay inside these ranges and needn't reach their ends.
All inputs are finite; a program needn't handle non-finite values.
Results may differ from the reference program's by a relative error of at most 0.0003.
Values sent between devices are 32-bit elements; how exact they have to be, the bound alone decides.
A program may use at most 64 MiB of HBM per device.

```python
import math
import jax
import jax.numpy as jnp
from jax import lax

D = 768
FF = 3072
RANK = 256
MATS = 4
NS_STEPS = 3
STEP = 10
VROWS = 13
LAYERS = 1


def scaled_gradient(seed_key, lead_shape, row_count, column_count):
    subkeys = jax.random.split(seed_key, 3)
    full_shape = lead_shape + (LAYERS, row_count, column_count)
    row_shape = lead_shape + (LAYERS, row_count, 1)
    column_shape = lead_shape + (LAYERS, 1, column_count)
    row_scale = jnp.exp(jax.random.uniform(subkeys[1], row_shape, jnp.float32) * math.log(10.0))
    column_scale = jnp.exp(jax.random.uniform(subkeys[2], column_shape, jnp.float32) * math.log(10.0))
    layer_place = jnp.arange(LAYERS, dtype=jnp.float32).reshape((LAYERS, 1, 1)) / max(LAYERS - 1, 1)
    layer_scale = 1.0 + 2.0 * layer_place
    entries = jnp.clip(jax.random.normal(subkeys[0], full_shape, jnp.float32), -5.0, 5.0)
    values = entries * row_scale * column_scale * layer_scale * 0.1
    return values.reshape(lead_shape + (LAYERS * row_count, column_count))


def draw_attention_grad(key, part):
    return scaled_gradient(jax.random.fold_in(key, 11), (MATS,), D, D).astype(jnp.bfloat16)


def draw_up_grad(key, part):
    return scaled_gradient(jax.random.fold_in(key, 12), (), D, FF).astype(jnp.bfloat16)


def draw_down_grad(key, part):
    return scaled_gradient(jax.random.fold_in(key, 13), (), FF, D).astype(jnp.bfloat16)


def shard_levels(key, extent, cuts, smallest, high):
    factor_of = 1.0
    for position, shards_of in cuts:
        draws = jax.random.uniform(jax.random.fold_in(jax.random.fold_in(key, 6), position), (shards_of,), jnp.float32, smallest / len(cuts), high / len(cuts))
        factor_of = factor_of * jnp.repeat(jnp.exp(draws), extent[position] // shards_of).reshape((-1,) + (1,) * (len(extent) - 1 - position))
    return factor_of


def centred(own_key, shape, scale, bound, cuts=(), kind=jnp.bfloat16):
    loudness = shard_levels(own_key, shape, cuts, -0.22, 0.18) if cuts else 1.0
    values = jax.random.normal(own_key, shape, jnp.float32) * scale * loudness
    return jnp.minimum(jnp.maximum(values, -bound), bound).astype(kind)


def setup_inputs(seed: int = 0) -> dict:
    arg_keys = jax.random.split(jax.random.key(seed), 16)
    return {
        "attention_grad": draw_attention_grad(jax.random.fold_in(arg_keys[15], 71), 0),
        "up_grad": draw_up_grad(jax.random.fold_in(arg_keys[15], 71), 0),
        "down_grad": draw_down_grad(jax.random.fold_in(arg_keys[15], 71), 0),
        "attention_basis": centred(arg_keys[3], (MATS, LAYERS * D, RANK), D ** -0.5, 0.21875, ((1, 8),), jnp.float32),
        "up_basis": centred(arg_keys[4], (LAYERS * D, RANK), D ** -0.5, 0.21875, ((0, 8),), jnp.float32),
        "down_basis": centred(arg_keys[5], (LAYERS * FF, RANK), FF ** -0.5, 0.109375, ((0, 8),), jnp.float32),
        "attention_mean": centred(arg_keys[6], (MATS, LAYERS * RANK, D), 0.3, 1.8, ((1, 8), (2, 4)), jnp.float32),
        "attention_power": jnp.clip(jnp.exp(math.log(1.0) - 2.9957323 * jax.random.uniform(arg_keys[7], (MATS, LAYERS * RANK, D), jnp.float32) ** shard_levels(arg_keys[7], (MATS, LAYERS * RANK, D), ((1, 8), (2, 4)), -0.2, 0.2)), 0.05, 1.0),
        "up_mean": centred(arg_keys[8], (LAYERS * RANK, FF), 0.3, 1.8, ((0, 8), (1, 4)), jnp.float32),
        "up_power": jnp.clip(jnp.exp(math.log(1.0) - 2.9957323 * jax.random.uniform(arg_keys[9], (LAYERS * RANK, FF), jnp.float32) ** shard_levels(arg_keys[9], (LAYERS * RANK, FF), ((0, 8), (1, 4)), -0.2, 0.2)), 0.05, 1.0),
        "down_mean": centred(arg_keys[10], (LAYERS * RANK, D), 0.3, 1.8, ((0, 8), (1, 4)), jnp.float32),
        "down_power": jnp.clip(jnp.exp(math.log(1.0) - 2.9957323 * jax.random.uniform(arg_keys[11], (LAYERS * RANK, D), jnp.float32) ** shard_levels(arg_keys[11], (LAYERS * RANK, D), ((0, 8), (1, 4)), -0.2, 0.2)), 0.05, 1.0),
        "vector_grad": centred(arg_keys[12], (VROWS, LAYERS * D), 1.0, 6.0, ((1, 32),), jnp.float32),
        "vector_mean": centred(arg_keys[13], (VROWS, LAYERS * D), 0.3, 1.8, ((1, 32),), jnp.float32),
        "vector_power": jnp.clip(jnp.exp(math.log(1.0) - 2.9957323 * jax.random.uniform(arg_keys[14], (VROWS, LAYERS * D), jnp.float32) ** shard_levels(arg_keys[14], (VROWS, LAYERS * D), ((1, 32),), -0.2, 0.2)), 0.05, 1.0),
    }


quintic_one = 3.4445
quintic_two = -4.775
quintic_three = 2.0315
decay_first = 0.9
decay_second = 0.95
adam_epsilon = 1e-08
norm_epsilon = 1e-07
galore_scale = 0.25
clip_rms = 1.0

def highest(left_side, right_side):
    return jnp.dot(left_side, right_side, precision=lax.Precision.HIGHEST, preferred_element_type=jnp.float32)

def quintic(gram_matrix):
    square = highest(gram_matrix, gram_matrix)
    identity = jnp.eye(gram_matrix.shape[0], dtype=jnp.float32)
    return quintic_one * identity + quintic_two * gram_matrix + quintic_three * square

def adam_moments(gradient, mean_now, power_now):
    mean_next = decay_first * mean_now + (1.0 - decay_first) * gradient
    power_next = decay_second * power_now + (1.0 - decay_second) * gradient * gradient
    fix_first = 1.0 - decay_first ** STEP
    fix_second = 1.0 - decay_second ** STEP
    normed = mean_next / fix_first / (jnp.sqrt(power_next / fix_second) + adam_epsilon)
    return (normed, mean_next, power_next)

def refine(gradient, basis, mean_now, power_now, factor):
    gradient = gradient.astype(jnp.float32) * factor
    projected = highest(basis.T, gradient)
    normed, mean_next, power_next = adam_moments(projected, mean_now, power_now)
    update = galore_scale * highest(basis, normed)
    subspace = highest(gradient, projected.T)
    gram_matrix = highest(subspace.T, subspace)
    scale_now = 1.0 / (jnp.sqrt(jnp.trace(gram_matrix)) + norm_epsilon)
    frame = subspace * scale_now
    gram_matrix = gram_matrix * (scale_now * scale_now)
    for sweep_index in range(NS_STEPS):
        frame = highest(frame, quintic(gram_matrix))
        gram_matrix = highest(frame.T, frame)
    return (update, mean_next, power_next, frame)

def reference(attention_grad, up_grad, down_grad, attention_basis, up_basis, down_basis, attention_mean, attention_power, up_mean, up_power, down_mean, down_power, vector_grad, vector_mean, vector_power):
    total_squares = jnp.sum(jnp.square(attention_grad.astype(jnp.float32)))
    total_squares = total_squares + jnp.sum(jnp.square(up_grad.astype(jnp.float32)))
    total_squares = total_squares + jnp.sum(jnp.square(down_grad.astype(jnp.float32)))
    total_squares = total_squares + jnp.sum(vector_grad * vector_grad)
    entry_count = LAYERS * (MATS * D * D + 2 * D * FF + VROWS * D)
    clip_limit = jnp.float32(clip_rms * math.sqrt(entry_count))
    factor = clip_limit / jnp.maximum(jnp.sqrt(total_squares), clip_limit)
    head_lists = [[[], [], [], []] for matrix in range(MATS)]
    up_lists = [[], [], [], []]
    down_lists = [[], [], [], []]
    for layer in range(LAYERS):
        row_low = layer * D
        rank_low = layer * RANK
        ff_low = layer * FF
        for matrix in range(MATS):
            result = refine(attention_grad[matrix, row_low:row_low + D], attention_basis[matrix, row_low:row_low + D], attention_mean[matrix, rank_low:rank_low + RANK], attention_power[matrix, rank_low:rank_low + RANK], factor)
            for slot in range(4):
                head_lists[matrix][slot].append(result[slot])
        result = refine(up_grad[row_low:row_low + D], up_basis[row_low:row_low + D], up_mean[rank_low:rank_low + RANK], up_power[rank_low:rank_low + RANK], factor)
        for slot in range(4):
            up_lists[slot].append(result[slot])
        result = refine(down_grad[ff_low:ff_low + FF], down_basis[ff_low:ff_low + FF], down_mean[rank_low:rank_low + RANK], down_power[rank_low:rank_low + RANK], factor)
        for slot in range(4):
            down_lists[slot].append(result[slot])

    def heads(slot):
        return jnp.stack([jnp.concatenate(head_lists[matrix][slot], 0) for matrix in range(MATS)], 0)
    step_vector, mean_vector, power_vector = adam_moments(vector_grad * factor, vector_mean, vector_power)
    return (heads(0), jnp.concatenate(up_lists[0], 0), jnp.concatenate(down_lists[0], 0), heads(1), heads(2), jnp.concatenate(up_lists[1], 0), jnp.concatenate(up_lists[2], 0), jnp.concatenate(down_lists[1], 0), jnp.concatenate(down_lists[2], 0), heads(3), jnp.concatenate(up_lists[3], 0), jnp.concatenate(down_lists[3], 0), step_vector, mean_vector, power_vector)
```

```python
import math

import jax
import jax.numpy as jnp
from jax import lax
from jax.sharding import PartitionSpec as P

NS_STEPS = 3
STEP = 10
GROUP = 8


quintic_one = 3.4445
quintic_two = -4.775
quintic_three = 2.0315
decay_first = 0.9
decay_second = 0.95
adam_epsilon = 1e-08
norm_epsilon = 1e-07
galore_scale = 0.25
clip_rms = 1.0


def partner(value, axis, stride):
    mask = 2**stride
    pairs = [(source, source ^ mask) for source in range(lax.axis_size(axis))]
    return lax.ppermute(value, axis, pairs)


def highest(left_side, right_side):
    return jnp.dot(
        left_side, right_side, precision=lax.Precision.HIGHEST, preferred_element_type=jnp.float32
    )


def contract(left_side, right_side, left_dim, right_dim):
    return lax.dot_general(
        left_side,
        right_side,
        (((left_dim,), (right_dim,)), ((), ())),
        precision=lax.Precision.HIGHEST,
        preferred_element_type=jnp.float32,
    )


def quintic(gram_matrix):
    square = highest(gram_matrix, gram_matrix)
    identity = jnp.eye(gram_matrix.shape[0], dtype=jnp.float32)
    return quintic_one * identity + quintic_two * gram_matrix + quintic_three * square


def adam_moments(gradient, mean_now, power_now):
    mean_next = decay_first * mean_now + (1.0 - decay_first) * gradient
    power_next = decay_second * power_now + (1.0 - decay_second) * gradient * gradient
    fix_first = 1.0 - decay_first**STEP
    fix_second = 1.0 - decay_second**STEP
    normed = mean_next / fix_first / (jnp.sqrt(power_next / fix_second) + adam_epsilon)
    return (normed, mean_next, power_next)


def bits_of(count):
    return count.bit_length() - 1


def relative_blocks(blocks, place):
    return jnp.concatenate(
        [
            lax.dynamic_index_in_dim(blocks, jnp.bitwise_xor(place, k), 0)
            for k in range(blocks.shape[0])
        ],
        0,
    )


def scatter_sum(blocks, axis):
    for bit_index in range(bits_of(blocks.shape[0])):
        half = blocks.reshape((-1, 2) + blocks.shape[1:])
        blocks = half[:, 0] + partner(half[:, 1], axis, bit_index)
    return blocks[0]


def gather_blocks(block, axis, count):
    blocks = block[None]
    for bit_index in reversed(range(bits_of(count))):
        received = partner(blocks, axis, bit_index)
        blocks = jnp.stack([blocks, received], 1).reshape((-1,) + block.shape)
    return blocks


def split_columns(block, widths):
    pieces = []
    column_start = 0
    for width in widths:
        pieces.append(block[..., column_start : column_start + width])
        column_start = column_start + width
    return pieces


def on_device(
    attention_grad,
    up_grad,
    down_grad,
    attention_basis,
    up_basis,
    down_basis,
    attention_mean,
    attention_power,
    up_mean,
    up_power,
    down_mean,
    down_power,
    vector_grad,
    vector_mean,
    vector_power,
):
    head_count = attention_grad.shape[0]
    matrix_count = head_count + 2
    gradients = [attention_grad[matrix].astype(jnp.float32) for matrix in range(head_count)]
    gradients = gradients + [up_grad.astype(jnp.float32), down_grad.astype(jnp.float32)]
    basis_list = [attention_basis[matrix] for matrix in range(head_count)] + [up_basis, down_basis]
    widths = [single.shape[1] for single in gradients]
    row_counts = [single.shape[0] for single in gradients]

    group_place = lax.axis_index("shard") % GROUP
    tensor_count = lax.axis_size("tensor")
    tensor_place = lax.axis_index("tensor")
    rank = attention_basis.shape[-1]
    block_rows = rank // GROUP
    rank_block = rank // tensor_count

    def clip_factor():
        local_squares = jnp.sum(vector_grad * vector_grad)
        for single in gradients:
            local_squares = local_squares + jnp.sum(single * single)
        total_squares = jnp.full((8, 128), local_squares, jnp.float32)
        for axis in ("tensor", "shard"):
            for bit_index in range(bits_of(lax.axis_size(axis))):
                total_squares = total_squares + partner(total_squares, axis, bit_index)
        total_squares = total_squares[0, 0]
        local_entries = sum((single.size for single in gradients)) + vector_grad.size
        entry_count = local_entries * lax.axis_size("shard") * lax.axis_size("tensor")
        clip_limit = jnp.float32(clip_rms * math.sqrt(entry_count))
        return clip_limit / jnp.maximum(jnp.sqrt(total_squares), clip_limit)

    factor = clip_factor()
    turned = jnp.concatenate(basis_list, 0).T.reshape(GROUP, block_rows, -1)
    turned = relative_blocks(turned, group_place).reshape(rank, -1)
    turned_list = split_columns(turned, row_counts)
    partial_term = jnp.concatenate(
        [highest(turned_list[matrix], gradients[matrix]) for matrix in range(matrix_count)], 1
    )
    own_rows = scatter_sum(partial_term.reshape(GROUP, block_rows, -1), "shard") * factor
    mean_now = jnp.concatenate(
        [attention_mean[matrix] for matrix in range(head_count)] + [up_mean, down_mean], 1
    )
    power_now = jnp.concatenate(
        [attention_power[matrix] for matrix in range(head_count)] + [up_power, down_power], 1
    )
    full_sums = gather_blocks(own_rows, "shard", GROUP).reshape(rank, -1)
    normed, mean_next, power_next = adam_moments(own_rows, mean_now, power_now)
    normed, full_sums = lax.optimization_barrier((normed, full_sums))
    full_normed = gather_blocks(normed, "shard", GROUP).reshape(rank, -1)
    sums_list = split_columns(full_sums, widths)
    mean_parts = split_columns(mean_next, widths)
    power_parts = split_columns(power_next, widths)
    mean_attention = jnp.stack(mean_parts[:head_count], 0)
    power_attention = jnp.stack(power_parts[:head_count], 0)

    partial_rows = jnp.concatenate(
        [contract(sums_list[matrix], gradients[matrix], 1, 1) for matrix in range(matrix_count)], 1
    )
    partial_rows = relative_blocks(partial_rows.reshape(GROUP, block_rows, -1), group_place)
    partial_rows = relative_blocks(
        partial_rows.reshape(tensor_count, rank_block, -1), tensor_place
    )
    own_block = scatter_sum(partial_rows, "tensor") * factor
    subspaces = gather_blocks(own_block, "tensor", tensor_count)
    subspaces = relative_blocks(subspaces, tensor_place).reshape(rank, -1)
    subspace_list = split_columns(subspaces, row_counts)
    own_list = split_columns(own_block, row_counts)

    gram_blocks = [
        contract(own_list[matrix], subspace_list[matrix], 1, 1) for matrix in range(matrix_count)
    ]
    gram_blocks = jnp.stack(
        gram_blocks + [jnp.zeros_like(gram_blocks[0])] * (GROUP - matrix_count), 0
    )
    gram_block = scatter_sum(relative_blocks(gram_blocks, group_place), "shard")
    gram_matrix = gather_blocks(gram_block, "tensor", tensor_count)
    gram_matrix = relative_blocks(gram_matrix, tensor_place).reshape(rank, rank)
    scale = 1.0 / (jnp.sqrt(jnp.trace(gram_matrix)) + norm_epsilon)
    gram_matrix = gram_matrix * (scale * scale)
    product = None
    for sweep_index in range(NS_STEPS):
        polynomial = quintic(gram_matrix)
        product = polynomial * scale if product is None else highest(product, polynomial)
        if sweep_index + 1 < NS_STEPS:
            gram_matrix = highest(polynomial, highest(gram_matrix, polynomial))
    own_product = lax.dynamic_index_in_dim(
        product.reshape(tensor_count, rank_block, rank), tensor_place, 0, keepdims=False
    )
    products = gather_blocks(own_product, "shard", GROUP)
    products = relative_blocks(products, group_place)[:matrix_count]
    products = relative_blocks(gather_blocks(products, "tensor", tensor_count), tensor_place)
    frames = [
        contract(subspace_list[matrix], products[:, matrix].reshape(rank, rank), 0, 0)
        for matrix in range(matrix_count)
    ]
    normed_list = split_columns(full_normed, widths)
    updates = [
        galore_scale * contract(turned_list[matrix], normed_list[matrix], 0, 0)
        for matrix in range(matrix_count)
    ]
    step_attention = jnp.stack(updates[:head_count], 0)
    step_up = updates[head_count]
    step_down = updates[head_count + 1]
    basis_attention = jnp.stack(frames[:head_count], 0)
    basis_up = frames[head_count]
    basis_down = frames[head_count + 1]
    step_vector, mean_vector, power_vector = adam_moments(
        vector_grad * factor, vector_mean, vector_power
    )
    return (
        step_attention,
        step_up,
        step_down,
        mean_attention,
        power_attention,
        mean_parts[head_count],
        power_parts[head_count],
        mean_parts[head_count + 1],
        power_parts[head_count + 1],
        basis_attention,
        basis_up,
        basis_down,
        step_vector,
        mean_vector,
        power_vector,
    )


def solution(mesh):
    in_specs = (
        P(None, "shard", "tensor"),
        P("shard", "tensor"),
        P("shard", "tensor"),
        P(None, "shard", None),
        P("shard", None),
        P("shard", None),
        P(None, "shard", "tensor"),
        P(None, "shard", "tensor"),
        P("shard", "tensor"),
        P("shard", "tensor"),
        P("shard", "tensor"),
        P("shard", "tensor"),
        P(None, ("shard", "tensor")),
        P(None, ("shard", "tensor")),
        P(None, ("shard", "tensor")),
    )
    out_specs = (
        P(None, "shard", "tensor"),
        P("shard", "tensor"),
        P("shard", "tensor"),
        P(None, "shard", "tensor"),
        P(None, "shard", "tensor"),
        P("shard", "tensor"),
        P("shard", "tensor"),
        P("shard", "tensor"),
        P("shard", "tensor"),
        P(None, "shard", None),
        P("shard", None),
        P("shard", None),
        P(None, ("shard", "tensor")),
        P(None, ("shard", "tensor")),
        P(None, ("shard", "tensor")),
    )
    return jax.shard_map(
        on_device, mesh=mesh, in_specs=in_specs, out_specs=out_specs, check_vma=False
    )
```

```python
import math

import jax
import jax.numpy as jnp
from jax import lax
from jax.sharding import PartitionSpec as P

NS_STEPS = 3
STEP = 10
GROUP = 8


quintic_one = 3.4445
quintic_two = -4.775
quintic_three = 2.0315
decay_first = 0.9
decay_second = 0.95
adam_epsilon = 1e-08
norm_epsilon = 1e-07
galore_scale = 0.25
clip_rms = 1.0


def partner(value, axis, stride):
    mask = 2**stride
    pairs = [(source, source ^ mask) for source in range(lax.axis_size(axis))]
    return lax.ppermute(value, axis, pairs)


def highest(left_side, right_side):
    return jnp.dot(
        left_side, right_side, precision=lax.Precision.HIGHEST, preferred_element_type=jnp.float32
    )


def contract(left_side, right_side, left_dim, right_dim):
    return lax.dot_general(
        left_side,
        right_side,
        (((left_dim,), (right_dim,)), ((), ())),
        precision=lax.Precision.HIGHEST,
        preferred_element_type=jnp.float32,
    )


def quintic(gram_matrix):
    square = highest(gram_matrix, gram_matrix)
    identity = jnp.eye(gram_matrix.shape[0], dtype=jnp.float32)
    return quintic_one * identity + quintic_two * gram_matrix + quintic_three * square


def adam_moments(gradient, mean_now, power_now):
    mean_next = decay_first * mean_now + (1.0 - decay_first) * gradient
    power_next = decay_second * power_now + (1.0 - decay_second) * gradient * gradient
    fix_first = 1.0 - decay_first**STEP
    fix_second = 1.0 - decay_second**STEP
    normed = mean_next / fix_first / (jnp.sqrt(power_next / fix_second) + adam_epsilon)
    return (normed, mean_next, power_next)


def bits_of(count):
    return count.bit_length() - 1


def relative_blocks(blocks, place):
    return jnp.concatenate(
        [
            lax.dynamic_index_in_dim(blocks, jnp.bitwise_xor(place, k), 0)
            for k in range(blocks.shape[0])
        ],
        0,
    )


def scatter_sum(blocks, axis):
    for bit_index in range(bits_of(blocks.shape[0])):
        half = blocks.reshape((-1, 2) + blocks.shape[1:])
        blocks = half[:, 0] + partner(half[:, 1], axis, bit_index)
    return blocks[0]


def gather_blocks(block, axis, count):
    blocks = block[None]
    for bit_index in reversed(range(bits_of(count))):
        blocks = widen(blocks, axis, bit_index)
    return blocks


def widen(blocks, axis, bit_index):
    received = partner(blocks, axis, bit_index)
    return jnp.stack([blocks, received], 1).reshape((-1,) + blocks.shape[1:])


def split_columns(block, widths):
    pieces = []
    column_start = 0
    for width in widths:
        pieces.append(block[..., column_start : column_start + width])
        column_start = column_start + width
    return pieces


def on_device(
    attention_grad,
    up_grad,
    down_grad,
    attention_basis,
    up_basis,
    down_basis,
    attention_mean,
    attention_power,
    up_mean,
    up_power,
    down_mean,
    down_power,
    vector_grad,
    vector_mean,
    vector_power,
):
    head_count = attention_grad.shape[0]
    matrix_count = head_count + 2
    gradients = [attention_grad[matrix].astype(jnp.float32) for matrix in range(head_count)]
    gradients = gradients + [up_grad.astype(jnp.float32), down_grad.astype(jnp.float32)]
    basis_list = [attention_basis[matrix] for matrix in range(head_count)] + [up_basis, down_basis]
    widths = [single.shape[1] for single in gradients]
    row_counts = [single.shape[0] for single in gradients]

    group_place = lax.axis_index("shard") % GROUP
    tensor_count = lax.axis_size("tensor")
    tensor_place = lax.axis_index("tensor")
    rank = attention_basis.shape[-1]
    block_rows = rank // GROUP
    rank_block = rank // tensor_count

    def clip_factor():
        local_squares = jnp.sum(vector_grad * vector_grad)
        for single in gradients:
            local_squares = local_squares + jnp.sum(single * single)
        total_squares = jnp.full((8, 128), local_squares, jnp.float32)
        for axis in ("tensor", "shard"):
            for bit_index in range(bits_of(lax.axis_size(axis))):
                total_squares = total_squares + partner(total_squares, axis, bit_index)
        total_squares = total_squares[0, 0]
        local_entries = sum((single.size for single in gradients)) + vector_grad.size
        entry_count = local_entries * lax.axis_size("shard") * lax.axis_size("tensor")
        clip_limit = jnp.float32(clip_rms * math.sqrt(entry_count))
        return clip_limit / jnp.maximum(jnp.sqrt(total_squares), clip_limit)

    factor = clip_factor()
    turned = jnp.concatenate(basis_list, 0).T.reshape(GROUP, block_rows, -1)
    turned = relative_blocks(turned, group_place).reshape(rank, -1)
    turned_list = split_columns(turned, row_counts)
    partial_term = jnp.concatenate(
        [highest(turned_list[matrix], gradients[matrix]) for matrix in range(matrix_count)], 1
    )
    own_rows = scatter_sum(partial_term.reshape(GROUP, block_rows, -1), "shard") * factor
    mean_now = jnp.concatenate(
        [attention_mean[matrix] for matrix in range(head_count)] + [up_mean, down_mean], 1
    )
    power_now = jnp.concatenate(
        [attention_power[matrix] for matrix in range(head_count)] + [up_power, down_power], 1
    )
    normed, mean_next, power_next = adam_moments(own_rows, mean_now, power_now)
    full_sums = own_rows[None]
    for bit_index in reversed(range(1, bits_of(GROUP))):
        full_sums = widen(full_sums, "shard", bit_index)
    full_normed, full_sums = lax.optimization_barrier((normed[None], full_sums))
    full_sums = widen(full_sums, "shard", 0)
    full_normed = widen(full_normed, "shard", 2)
    full_normed, full_sums = lax.optimization_barrier((full_normed, full_sums))
    full_sums = full_sums.reshape(rank, -1)
    full_normed = widen(full_normed, "shard", 1)
    sums_list = split_columns(full_sums, widths)
    mean_parts = split_columns(mean_next, widths)
    power_parts = split_columns(power_next, widths)
    mean_attention = jnp.stack(mean_parts[:head_count], 0)
    power_attention = jnp.stack(power_parts[:head_count], 0)

    partial_rows = jnp.concatenate(
        [contract(sums_list[matrix], gradients[matrix], 1, 1) for matrix in range(matrix_count)], 1
    )
    partial_rows = relative_blocks(partial_rows.reshape(GROUP, block_rows, -1), group_place)
    partial_rows = relative_blocks(
        partial_rows.reshape(tensor_count, rank_block, -1), tensor_place
    )
    own_block = scatter_sum(partial_rows, "tensor") * factor
    full_normed, own_block = lax.optimization_barrier((full_normed, own_block))
    full_normed = widen(full_normed, "shard", 0)
    subspaces = gather_blocks(own_block, "tensor", tensor_count)
    subspaces = relative_blocks(subspaces, tensor_place).reshape(rank, -1)
    subspace_list = split_columns(subspaces, row_counts)
    own_list = split_columns(own_block, row_counts)

    gram_blocks = [
        contract(own_list[matrix], subspace_list[matrix], 1, 1) for matrix in range(matrix_count)
    ]
    gram_blocks = jnp.stack(
        gram_blocks + [jnp.zeros_like(gram_blocks[0])] * (GROUP - matrix_count), 0
    )
    gram_block = scatter_sum(relative_blocks(gram_blocks, group_place), "shard")
    full_normed, gram_block = lax.optimization_barrier((full_normed, gram_block))
    full_normed = full_normed.reshape(rank, -1)
    gram_matrix = gather_blocks(gram_block, "tensor", tensor_count)
    gram_matrix = relative_blocks(gram_matrix, tensor_place).reshape(rank, rank)
    scale = 1.0 / (jnp.sqrt(jnp.trace(gram_matrix)) + norm_epsilon)
    gram_matrix = gram_matrix * (scale * scale)
    product = None
    for sweep_index in range(NS_STEPS):
        polynomial = quintic(gram_matrix)
        product = polynomial * scale if product is None else highest(product, polynomial)
        if sweep_index + 1 < NS_STEPS:
            gram_matrix = highest(polynomial, highest(gram_matrix, polynomial))
    own_product = lax.dynamic_index_in_dim(
        product.reshape(tensor_count, rank_block, rank), tensor_place, 0, keepdims=False
    )
    products = gather_blocks(own_product, "shard", GROUP)
    products = relative_blocks(products, group_place)[:matrix_count]
    products = relative_blocks(gather_blocks(products, "tensor", tensor_count), tensor_place)
    frames = [
        contract(subspace_list[matrix], products[:, matrix].reshape(rank, rank), 0, 0)
        for matrix in range(matrix_count)
    ]
    normed_list = split_columns(full_normed, widths)
    updates = [
        galore_scale * contract(turned_list[matrix], normed_list[matrix], 0, 0)
        for matrix in range(matrix_count)
    ]
    step_attention = jnp.stack(updates[:head_count], 0)
    step_up = updates[head_count]
    step_down = updates[head_count + 1]
    basis_attention = jnp.stack(frames[:head_count], 0)
    basis_up = frames[head_count]
    basis_down = frames[head_count + 1]
    step_vector, mean_vector, power_vector = adam_moments(
        vector_grad * factor, vector_mean, vector_power
    )
    return (
        step_attention,
        step_up,
        step_down,
        mean_attention,
        power_attention,
        mean_parts[head_count],
        power_parts[head_count],
        mean_parts[head_count + 1],
        power_parts[head_count + 1],
        basis_attention,
        basis_up,
        basis_down,
        step_vector,
        mean_vector,
        power_vector,
    )


def solution(mesh):
    in_specs = (
        P(None, "shard", "tensor"),
        P("shard", "tensor"),
        P("shard", "tensor"),
        P(None, "shard", None),
        P("shard", None),
        P("shard", None),
        P(None, "shard", "tensor"),
        P(None, "shard", "tensor"),
        P("shard", "tensor"),
        P("shard", "tensor"),
        P("shard", "tensor"),
        P("shard", "tensor"),
        P(None, ("shard", "tensor")),
        P(None, ("shard", "tensor")),
        P(None, ("shard", "tensor")),
    )
    out_specs = (
        P(None, "shard", "tensor"),
        P("shard", "tensor"),
        P("shard", "tensor"),
        P(None, "shard", "tensor"),
        P(None, "shard", "tensor"),
        P("shard", "tensor"),
        P("shard", "tensor"),
        P("shard", "tensor"),
        P("shard", "tensor"),
        P(None, "shard", None),
        P("shard", None),
        P("shard", None),
        P(None, ("shard", "tensor")),
        P(None, ("shard", "tensor")),
        P(None, ("shard", "tensor")),
    )
    return jax.shard_map(
        on_device, mesh=mesh, in_specs=in_specs, out_specs=out_specs, check_vma=False
    )
```
